32 devices in a mesh: groups: 2 (over y), blk: 8 (over z, x), uly: 2 (over core).
Axes of the slice: x: 2, y: 2, z: 4, core: 2. Of those that a mesh axis runs over, the one named last changes fastest.
Arguments:
- query: bfloat16 [4096, 1536], P(('groups', 'blk', 'uly')), parts along dimension 0, may hold values from -12 to 12
- key: bfloat16 [4096, 1536], P(('groups', 'blk', 'uly')), parts along dimension 0, may hold values from -6 to 6
- value: bfloat16 [4096, 1536], P(('groups', 'blk', 'uly')), parts along dimension 0, may hold values from -6 to 6
- keep: int32 [64, 28], P(('groups', 'blk')), parts along dimension 0, may hold values from 0 to 1, as said below
Outputs:
- attended: bfloat16 [4096, 1536], P(('groups', 'blk', 'uly')), parts along dimension 0
The draws below stay inside these ranges and needn't reach their ends.
There are 2 independent parts, one for each index of `groups`. The reference program is written for one: setup_inputs(seed, part) draws one part's arguments, and reference() takes and returns one part's arrays. A program takes and returns all parts, laid end to end along the dimension named above; each array names one. Nothing has to cross between parts.
Inputs may be any that keep to these rules, and one draw needn't show every extreme that they name: Tile i has coordinates (i // 8, (i // 2) % 4, i % 2) in the clip's grid of tiles. keep[i, j] refers to key tile (i // 4 - 3) * 4 + j; it is 0 where that tile lies outside the clip, 1 where it is tile i itself, and otherwise 1 exactly when each coordinate differs from tile i's by no more than a per-tile reach of 0 or 1 in that coordinate.
All inputs are finite; a program needn't handle non-finite values.
Results may differ from the reference program's by a relative error of at most 0.0029.
Values may be sent and summed in bfloat16 or wider, within the bound.
A program may use at most 64 MiB of HBM per device.

```python
import math
import jax
import jax.numpy as jnp
from jax import lax

HEADS = 12
HD = 128
TILE = 64
TH = 4
TW = 2
QBLK = 256
TILES_BLK = 4
RADIUS = 3
BAND = 28
SEQ = 2048
NTILES = 32
N_BLK = 8


def draw_query(key, part):
    noise_key = jax.random.fold_in(key, 1)
    base = jnp.clip(3.0 * jax.random.normal(noise_key, (SEQ, HEADS * HD), jnp.float32), -12.0, 12.0)
    return base.astype(jnp.bfloat16)


def draw_key(key, part):
    noise_key = jax.random.fold_in(key, 2)
    base = jnp.clip(jax.random.normal(noise_key, (SEQ, HEADS * HD), jnp.float32), -6.0, 6.0)
    return base.astype(jnp.bfloat16)


def draw_keep(key, part):
    tiles = jnp.arange(NTILES, dtype=jnp.int32)[:, None]
    column = jnp.arange(BAND, dtype=jnp.int32)[None, :]
    other = (tiles // TILES_BLK - RADIUS) * TILES_BLK + column
    reaches = jax.random.randint(jax.random.fold_in(key, 3), (3, NTILES, 1), 0, 2)
    plane = TH * TW
    near_t = jnp.abs(tiles // plane - other // plane) <= reaches[0]
    near_h = jnp.abs(tiles // TW % TH - other // TW % TH) <= reaches[1]
    near_w = jnp.abs(tiles % TW - other % TW) <= reaches[2]
    inside = (other >= 0) & (other < NTILES)
    return (near_t & near_h & near_w & inside).astype(jnp.int32)


def shard_levels(own_key, extent, shards, smallest, largest):
    factor_of, own = 1.0, jax.random.fold_in(own_key, 6)
    for dim, blocks in shards:
        steps = jnp.exp(jax.random.uniform(jax.random.fold_in(own, dim), (blocks,), jnp.float32, smallest / len(shards), largest / len(shards)))
        factor_of = factor_of * jnp.repeat(steps, extent[dim] // blocks).reshape([-1 if axis == dim else 1 for axis in range(len(extent))])
    return factor_of


def scatter_about(key, dims, width, limit, shards=(), held_as=jnp.bfloat16):
    level = shard_levels(key, dims, shards, -0.22, 0.18) if shards else 1.0
    drawn = jax.random.normal(key, dims, jnp.float32) * width * level
    return jnp.minimum(jnp.maximum(drawn, -limit), limit).astype(held_as)


def setup_inputs(seed: int = 0, part: int = 0) -> dict:
    splits = jax.random.split(jax.random.key(seed), 5)
    part_splits = jax.random.split(jax.random.fold_in(splits[4], part), 5)
    query = draw_query(jax.random.fold_in(jax.random.fold_in(splits[4], part), 71), part)
    key = draw_key(jax.random.fold_in(jax.random.fold_in(splits[4], part), 71), part)
    value = scatter_about(part_splits[2], (SEQ, HEADS * HD), 1.0, 6.0, ((0, 16),))
    keep = draw_keep(jax.random.fold_in(jax.random.fold_in(splits[4], part), 71), part)
    return {"query": query, "key": key, "value": value, "keep": keep}


def reference(query, key, value, keep):
    scale = 1.0 / math.sqrt(HD)
    span = (2 * RADIUS + 1) * QBLK
    q_all = query.reshape(N_BLK, QBLK, HEADS, HD)
    padding = ((RADIUS * QBLK, RADIUS * QBLK), (0, 0))
    k_pad = jnp.pad(key, padding)
    v_pad = jnp.pad(value, padding)
    flags = keep.reshape(N_BLK, TILES_BLK, BAND)

    def one_block(block):
        q_blk = lax.dynamic_index_in_dim(q_all, block, 0, keepdims=False).astype(jnp.float32)
        begin = (block * QBLK).astype(jnp.int32)
        k_blk = lax.dynamic_slice_in_dim(k_pad, begin, span, 0).reshape(span, HEADS, HD).astype(jnp.float32)
        v_blk = lax.dynamic_slice_in_dim(v_pad, begin, span, 0).reshape(span, HEADS, HD).astype(jnp.float32)
        tile_flags = lax.dynamic_index_in_dim(flags, block, 0, keepdims=False) > 0
        mask = jnp.repeat(jnp.repeat(tile_flags, TILE, axis=0), TILE, axis=1)[:, None, :]
        scores = jnp.einsum('qhd,khd->qhk', q_blk, k_blk) * scale
        masked = jnp.where(mask, scores, -1e+30)
        peak = lax.optimization_barrier(jnp.max(masked, axis=2, keepdims=True))
        weights = jnp.where(mask, jnp.exp(masked - peak), 0.0)
        total = lax.optimization_barrier(jnp.sum(weights, axis=2))
        rounded = lax.optimization_barrier(weights.astype(jnp.bfloat16)).astype(jnp.float32)
        mixed = jnp.einsum('qhk,khd->qhd', rounded, v_blk) / total[:, :, None]
        return mixed.astype(jnp.bfloat16).reshape(QBLK, HEADS * HD)
    result = lax.map(one_block, jnp.arange(N_BLK, dtype=jnp.int32))
    return result.reshape(SEQ, HEADS * HD)
```

```python
import functools
import math

import jax
import jax.numpy as jnp
from jax import lax
from jax.experimental import pallas as pl
from jax.experimental.pallas import tpu as pltpu
from jax.sharding import PartitionSpec as P

HD = 128
TILE = 64
FAR = 1e30
F32 = jnp.float32
BF16 = jnp.bfloat16
MESH = pl.DeviceIdType.MESH


def kernel(heads, frames, query, key, value, keep, out,
           kv, kvs, qs, q2, fq, fkeep, bias, fbias, ps, pr, accs, peaks, totals, o2,
           sem_kvs, sem_qs, sem_own, sem_own_q, recv_kv, zsend, psend, pqsend, recv_q2,
           fqsend, recv_fq, ksend, recv_keep, part_send, part_recv, out_local, out_send, out_recv):
    half = heads // 2
    group = lax.axis_index("groups")
    b = lax.axis_index("blk")
    u = lax.axis_index("uly")
    t = b // 2
    s = b - 2 * t
    other = 1 - u
    facing = 1 - s
    across = b + 1 - 2 * s
    has_low = t > 0
    has_high = t < frames - 1

    def dev(blk, core):
        return (group, blk, core)

    def remote(src, dst, send, recv, device):
        return pltpu.make_async_remote_copy(
            src_ref=src, dst_ref=dst, send_sem=send, recv_sem=recv,
            device_id=device, device_id_type=MESH)

    def columns(head):
        return pl.ds(pl.multiple_of(head * HD, HD), HD)

    def load_key(hd):
        return pltpu.make_async_copy(key.at[:, columns(hd)], kvs.at[hd, 0], sem_kvs.at[hd, 0])

    def load_value(hd):
        return pltpu.make_async_copy(value.at[:, columns(hd)], kvs.at[hd, 1], sem_kvs.at[hd, 1])

    def load_query(hd):
        return pltpu.make_async_copy(query.at[:, columns(hd)], qs.at[hd], sem_qs.at[hd])

    def own_kv(h):
        return (
            pltpu.make_async_copy(key.at[:, columns(u * half + h)], kv.at[h, 2 + u, 0], sem_own.at[h, 0]),
            pltpu.make_async_copy(value.at[:, columns(u * half + h)], kv.at[h, 2 + u, 1], sem_own.at[h, 1]),
        )

    def own_q(h):
        return pltpu.make_async_copy(query.at[:, columns(u * half + h)], q2.at[h, u], sem_own_q.at[h])

    for h in range(half):
        for c in range(2):
            load_key(c * half + h).start()
            load_value(c * half + h).start()
            load_query(c * half + h).start()
    for h in range(half):
        for copy in own_kv(h):
            copy.start()
        own_q(h).start()

    def to_high(c, h):
        return remote(kvs.at[c * half + h], kv.at[h, u], zsend.at[0, c, h], recv_kv.at[u, h], dev(b + 2, c))

    def to_low(c, h):
        return remote(kvs.at[c * half + h], kv.at[h, 4 + u], zsend.at[1, c, h], recv_kv.at[4 + u, h], dev(b - 2, c))

    def got_kv(row, h):
        return remote(kvs.at[h], kv.at[h, row], zsend.at[0, 0, h], recv_kv.at[row, h], dev(b, other))

    def to_partner_kv():
        return remote(kvs.at[pl.ds(other * half, half)], kv.at[:, 2 + u], psend.at[0], psend.at[1], dev(b, other))

    def got_partner_kv():
        return remote(kvs.at[pl.ds(other * half, half)], kv.at[:, 2 + other], psend.at[0], psend.at[1], dev(b, other))

    def to_partner_q():
        return remote(qs.at[pl.ds(other * half, half)], q2.at[:, u], pqsend.at[0], recv_q2.at[0], dev(b, other))

    def got_partner_q():
        return remote(qs.at[pl.ds(other * half, half)], q2.at[:, other], pqsend.at[0], recv_q2.at[0], dev(b, other))

    def to_across_q(c, h):
        return remote(qs.at[c * half + h], fq.at[h], fqsend.at[c, h], recv_fq.at[h], dev(across, c))

    def to_across_keep():
        return remote(keep, fkeep, ksend.at[0], recv_keep.at[0], dev(across, u))

    def part(h):
        return remote(ps.at[h], pr.at[h], part_send.at[h], part_recv.at[h], dev(across, u))

    barrier = pltpu.get_barrier_semaphore()

    def greet(blk, core):
        pl.semaphore_signal(barrier, inc=1, device_id=dev(blk, core), device_id_type=MESH)

    greet(b, other)
    for c in range(2):
        greet(across, c)

        @pl.when(has_low)
        def _(c=c):
            greet(b - 2, c)

        @pl.when(has_high)
        def _(c=c):
            greet(b + 2, c)

    @pl.when(jnp.logical_not(has_low))
    def _():
        kv[:, 0:2] = jnp.zeros((half, 2, 2, HD, HD), BF16)

    @pl.when(jnp.logical_not(has_high))
    def _():
        kv[:, 4:6] = jnp.zeros((half, 2, 2, HD, HD), BF16)

    around = jnp.where(has_low, 2, 0) + jnp.where(has_high, 2, 0)
    pl.semaphore_wait(barrier, 3 + around)

    to_across_keep().start()
    for h in range(half):
        for c in range(2):
            load_key(c * half + h).wait()
            load_value(c * half + h).wait()

            @pl.when(has_high)
            def _(c=c, h=h):
                to_high(c, h).start()

            @pl.when(has_low)
            def _(c=c, h=h):
                to_low(c, h).start()

            load_query(c * half + h).wait()

            @pl.when(u == facing)
            def _(c=c, h=h):
                to_across_q(c, h).start()

    to_partner_kv().start()
    to_partner_q().start()
    for h in range(half):
        for copy in own_kv(h):
            copy.wait()
        own_q(h).wait()

    wide = keep.shape[1]
    tiles_here = keep.shape[0]
    reach = (wide // tiles_here - 1) // 2

    def addend(flags, column, count):
        lanes = lax.broadcasted_iota(jnp.int32, (wide, count), 1)
        chosen = lax.broadcasted_iota(jnp.int32, (wide, count), 0) == column(lanes)
        picked = jnp.dot(flags.astype(F32).astype(BF16), chosen.astype(F32).astype(BF16), preferred_element_type=F32)
        return jnp.where(picked > 0.5, 0.0, -FAR)

    def own_column(lanes):
        row = lanes // HD
        return (tiles_here * (reach - 2) + 2 * tiles_here * (row // 2)
                + 2 * (row % 2) + (lanes % HD) // TILE)

    def far_column(lanes):
        return (tiles_here * (reach - 2 + 2 * s - 1) + 2 * tiles_here * (lanes // HD)
                + 2 * facing + (lanes % HD) // TILE)

    bias[...] = addend(keep[...], own_column, 6 * HD)
    remote(keep, fkeep, ksend.at[0], recv_keep.at[0], dev(across, u)).wait_recv()
    fbias[...] = addend(fkeep[...], far_column, 3 * HD)

    got_partner_kv().wait_recv()
    got_partner_q().wait_recv()

    scale = math.log2(math.e) / math.sqrt(HD)
    nt = (((1,), (1,)), ((), ()))

    def softmax(scores, rows, addends):
        ms, ls, ws = [], [], []
        for i in range(rows // TILE):
            x = scores[i * TILE:(i + 1) * TILE] * scale + addends[i]
            m = jnp.max(x, axis=1, keepdims=True)
            w = jnp.exp2(x - m)
            ls.append(jnp.sum(w, axis=1, keepdims=True))
            ms.append(m)
            ws.append(w.astype(BF16))
        return jnp.concatenate(ms, 0), jnp.concatenate(ls, 0), jnp.concatenate(ws, 0)

    def far(h):
        k = jnp.concatenate([kv[h, 2 * i + facing, 0] for i in range(3)], 0)
        v = jnp.concatenate([kv[h, 2 * i + facing, 1] for i in range(3)], 0)
        scores = lax.dot_general(fq[h], k, nt, preferred_element_type=F32)
        m, l, w = softmax(scores, HD, [fbias[pl.ds(2 * s + i, 1), :] for i in range(2)])
        ps[h, 0:HD, :] = jnp.dot(w, v, preferred_element_type=F32)
        lane = lax.broadcasted_iota(jnp.int32, (HD, HD), 1)
        ps[h, HD:HD + 8, :] = jnp.where(lane == 0, m, l).T[0:8, :]
        part(h).start()

    def near(h):
        k = kv[h, :, 0].reshape(6 * HD, HD)
        v = kv[h, :, 1].reshape(6 * HD, HD)
        scores = lax.dot_general(q2[h].reshape(2 * HD, HD), k, nt, preferred_element_type=F32)
        m, l, w = softmax(scores, 2 * HD, [bias[i:i + 1, :] for i in range(4)])
        accs[h] = jnp.dot(w, v, preferred_element_type=F32).reshape(2, HD, HD)
        peaks[h] = jnp.broadcast_to(m, (2 * HD, HD)).reshape(2, HD, HD)
        totals[h] = jnp.broadcast_to(l, (2 * HD, HD)).reshape(2, HD, HD)

    def keep_out(h):
        return pltpu.make_async_copy(o2.at[h, u], out.at[:, columns(u * half + h)], out_local.at[h])

    def give_out(h):
        return remote(o2.at[h, other], out.at[:, columns(u * half + h)], out_send.at[h], out_recv.at[h], dev(b, other))

    def got_out(h):
        return remote(o2.at[h, other], out.at[:, columns(other * half + h)], out_send.at[h], out_recv.at[h], dev(b, other))

    def merge(h):
        o2[h, s] = (accs[h, s] / totals[h, s]).astype(BF16)
        part(h).wait_recv()
        stats = jnp.concatenate([pr[h, HD:HD + 8, :]] * 16, 0).T
        m2, l2 = stats[:, 0:1], stats[:, 1:2]
        m1 = peaks[h, facing]
        m = jnp.maximum(m1, m2)
        a1, a2 = jnp.exp2(m1 - m), jnp.exp2(m2 - m)
        mixed = accs[h, facing] * a1 + pr[h, 0:HD, :] * a2
        o2[h, facing] = (mixed / (totals[h, facing] * a1 + l2 * a2)).astype(BF16)
        give_out(h).start()
        keep_out(h).start()

    def step(h, carry):
        for r in range(2):
            @pl.when(has_low)
            def _(r=r):
                got_kv(r, h).wait_recv()

            @pl.when(has_high)
            def _(r=r):
                got_kv(4 + r, h).wait_recv()

        to_across_q(0, h).wait_recv()
        far(h)
        near(h)

        @pl.when(h > 0)
        def _():
            merge(h - 1)

        return carry

    lax.fori_loop(0, half, step, 0)
    merge(half - 1)

    to_across_keep().wait_send()
    to_partner_kv().wait_send()
    to_partner_q().wait_send()
    for h in range(half):
        for c in range(2):
            @pl.when(has_high)
            def _(c=c, h=h):
                to_high(c, h).wait_send()

            @pl.when(has_low)
            def _(c=c, h=h):
                to_low(c, h).wait_send()

            @pl.when(u == facing)
            def _(c=c, h=h):
                to_across_q(c, h).wait_send()

        part(h).wait_send()
        keep_out(h).wait()
        give_out(h).wait_send()
        got_out(h).wait_recv()


def body(query, key, value, keep):
    rows, width = query.shape
    heads = width // HD
    half = heads // 2
    frames = lax.axis_size("blk") // 2
    tiles, span = keep.shape
    dma = pltpu.SemaphoreType.DMA
    anywhere = pl.BlockSpec(memory_space=pl.ANY)
    scratch = [
        pltpu.VMEM((half, 6, 2, HD, HD), BF16),
        pltpu.VMEM((heads, 2, HD, HD), BF16),
        pltpu.VMEM((heads, HD, HD), BF16),
        pltpu.VMEM((half, 2, HD, HD), BF16),
        pltpu.VMEM((half, HD, HD), BF16),
        pltpu.VMEM((tiles, span), jnp.int32),
        pltpu.VMEM((tiles, 6 * HD), F32),
        pltpu.VMEM((tiles, 3 * HD), F32),
        pltpu.VMEM((half, HD + 8, HD), F32),
        pltpu.VMEM((half, HD + 8, HD), F32),
        pltpu.VMEM((half, 2, HD, HD), F32),
        pltpu.VMEM((half, 2, HD, HD), F32),
        pltpu.VMEM((half, 2, HD, HD), F32),
        pltpu.VMEM((half, 2, HD, HD), BF16),
        dma((heads, 2)),
        dma((heads,)),
        dma((half, 2)),
        dma((half,)),
        dma((6, half)),
        dma((2, 2, half)),
        dma((2,)),
        dma((1,)),
        dma((1,)),
        dma((2, half)),
        dma((half,)),
        dma((1,)),
        dma((1,)),
        dma((half,)),
        dma((half,)),
        dma((half,)),
        dma((half,)),
        dma((half,)),
    ]
    return pl.pallas_call(
        functools.partial(kernel, heads, frames),
        out_shape=jax.ShapeDtypeStruct((rows, width), BF16),
        in_specs=[anywhere, anywhere, anywhere, pl.BlockSpec(memory_space=pltpu.VMEM)],
        out_specs=anywhere,
        scratch_shapes=scratch,
        compiler_params=pltpu.CompilerParams(
            collective_id=0, has_side_effects=True, vmem_limit_bytes=56 * 1024 * 1024),
    )(query, key, value, keep)


def solution(mesh):
    return jax.shard_map(
        body,
        mesh=mesh,
        in_specs=(
            P(("groups", "blk", "uly"), None),
            P(("groups", "blk", "uly"), None),
            P(("groups", "blk", "uly"), None),
            P(("groups", "blk"), None),
        ),
        out_specs=P(("groups", "blk", "uly"), None),
        check_vma=False,
    )
```

```python
import functools
import math

import jax
import jax.numpy as jnp
from jax import lax
from jax.experimental import pallas as pl
from jax.experimental.pallas import tpu as pltpu
from jax.sharding import PartitionSpec as P

HD = 128
TILE = 64
FAR = 1e30
LEAD = 4
F32 = jnp.float32
BF16 = jnp.bfloat16
MESH = pl.DeviceIdType.MESH


def kernel(heads, frames, query, key, value, keep, out,
           kv, kvs, qs, q2, fq, fkeep, bias, fbias, ps, pr, accs, peaks, totals, o2,
           sem_kvs, sem_qs, sem_own, sem_own_q, recv_kv, zsend, psend, pqsend, recv_q2,
           fqsend, recv_fq, ksend, recv_keep, part_send, part_recv, out_local, out_send, out_recv):
    half = heads // 2
    group = lax.axis_index("groups")
    b = lax.axis_index("blk")
    u = lax.axis_index("uly")
    t = b // 2
    s = b - 2 * t
    other = 1 - u
    facing = 1 - s
    across = b + 1 - 2 * s
    has_low = t > 0
    has_high = t < frames - 1

    def dev(blk, core):
        return (group, blk, core)

    def remote(src, dst, send, recv, device):
        return pltpu.make_async_remote_copy(
            src_ref=src, dst_ref=dst, send_sem=send, recv_sem=recv,
            device_id=device, device_id_type=MESH)

    def columns(head):
        return pl.ds(pl.multiple_of(head * HD, HD), HD)

    def load_key(hd):
        return pltpu.make_async_copy(key.at[:, columns(hd)], kvs.at[hd, 0], sem_kvs.at[hd, 0])

    def load_value(hd):
        return pltpu.make_async_copy(value.at[:, columns(hd)], kvs.at[hd, 1], sem_kvs.at[hd, 1])

    def load_query(hd):
        return pltpu.make_async_copy(query.at[:, columns(hd)], qs.at[hd], sem_qs.at[hd])

    def own_kv(h):
        return (
            pltpu.make_async_copy(key.at[:, columns(u * half + h)], kv.at[h, 2 + u, 0], sem_own.at[h, 0]),
            pltpu.make_async_copy(value.at[:, columns(u * half + h)], kv.at[h, 2 + u, 1], sem_own.at[h, 1]),
        )

    def own_q(h):
        return pltpu.make_async_copy(query.at[:, columns(u * half + h)], q2.at[h, u], sem_own_q.at[h])

    for h in range(half):
        for c in range(2):
            load_key(c * half + h).start()
            load_value(c * half + h).start()
            load_query(c * half + h).start()
    for h in range(half):
        for copy in own_kv(h):
            copy.start()
        own_q(h).start()

    def to_high(c, h):
        return remote(kvs.at[c * half + h], kv.at[h, u], zsend.at[0, c, h], recv_kv.at[u, h], dev(b + 2, c))

    def to_low(c, h):
        return remote(kvs.at[c * half + h], kv.at[h, 4 + u], zsend.at[1, c, h], recv_kv.at[4 + u, h], dev(b - 2, c))

    def got_kv(row, h):
        return remote(kvs.at[h], kv.at[h, row], zsend.at[0, 0, h], recv_kv.at[row, h], dev(b, other))

    def to_partner_kv():
        return remote(kvs.at[pl.ds(other * half, half)], kv.at[:, 2 + u], psend.at[0], psend.at[1], dev(b, other))

    def got_partner_kv():
        return remote(kvs.at[pl.ds(other * half, half)], kv.at[:, 2 + other], psend.at[0], psend.at[1], dev(b, other))

    def to_partner_q():
        return remote(qs.at[pl.ds(other * half, half)], q2.at[:, u], pqsend.at[0], recv_q2.at[0], dev(b, other))

    def got_partner_q():
        return remote(qs.at[pl.ds(other * half, half)], q2.at[:, other], pqsend.at[0], recv_q2.at[0], dev(b, other))

    def to_across_q(c, h):
        return remote(qs.at[c * half + h], fq.at[h], fqsend.at[c, h], recv_fq.at[h], dev(across, c))

    def to_across_keep():
        return remote(keep, fkeep, ksend.at[0], recv_keep.at[0], dev(across, u))

    def part(h):
        return remote(ps.at[h], pr.at[h], part_send.at[h], part_recv.at[h], dev(across, u))

    barrier = pltpu.get_barrier_semaphore()

    def greet(blk, core):
        pl.semaphore_signal(barrier, inc=1, device_id=dev(blk, core), device_id_type=MESH)

    greet(b, other)
    for c in range(2):
        greet(across, c)

        @pl.when(has_low)
        def _(c=c):
            greet(b - 2, c)

        @pl.when(has_high)
        def _(c=c):
            greet(b + 2, c)

    @pl.when(jnp.logical_not(has_low))
    def _():
        kv[:, 0:2] = jnp.zeros((half, 2, 2, HD, HD), BF16)

    @pl.when(jnp.logical_not(has_high))
    def _():
        kv[:, 4:6] = jnp.zeros((half, 2, 2, HD, HD), BF16)

    around = jnp.where(has_low, 2, 0) + jnp.where(has_high, 2, 0)
    pl.semaphore_wait(barrier, 3 + around)

    def send_kv(c, h):
        @pl.when(has_high)
        def _():
            to_high(c, h).start()

        @pl.when(has_low)
        def _():
            to_low(c, h).start()

    to_across_keep().start()
    for h in range(half):
        for c in range(2):
            load_key(c * half + h).wait()
            load_value(c * half + h).wait()

            @pl.when(u == facing)
            def _(c=c, h=h):
                send_kv(c, h)

            load_query(c * half + h).wait()

            @pl.when(u == facing)
            def _(c=c, h=h):
                to_across_q(c, h).start()

    to_partner_kv().start()
    to_partner_q().start()
    for h in range(half):
        for copy in own_kv(h):
            copy.wait()
        own_q(h).wait()

    wide = keep.shape[1]
    tiles_here = keep.shape[0]
    reach = (wide // tiles_here - 1) // 2

    def addend(flags, column, count):
        lanes = lax.broadcasted_iota(jnp.int32, (wide, count), 1)
        chosen = lax.broadcasted_iota(jnp.int32, (wide, count), 0) == column(lanes)
        picked = jnp.dot(flags.astype(F32).astype(BF16), chosen.astype(F32).astype(BF16), preferred_element_type=F32)
        return jnp.where(picked > 0.5, 0.0, -FAR)

    def own_column(lanes):
        row = lanes // HD
        return (tiles_here * (reach - 2) + 2 * tiles_here * (row // 2)
                + 2 * (row % 2) + (lanes % HD) // TILE)

    def far_column(lanes):
        return (tiles_here * (reach - 2 + 2 * s - 1) + 2 * tiles_here * (lanes // HD)
                + 2 * facing + (lanes % HD) // TILE)

    bias[...] = addend(keep[...], own_column, 6 * HD)
    remote(keep, fkeep, ksend.at[0], recv_keep.at[0], dev(across, u)).wait_recv()
    fbias[...] = addend(fkeep[...], far_column, 3 * HD)

    got_partner_kv().wait_recv()
    got_partner_q().wait_recv()

    scale = math.log2(math.e) / math.sqrt(HD)
    nt = (((1,), (1,)), ((), ()))

    def softmax(scores, rows, addends):
        ms, ls, ws = [], [], []
        for i in range(rows // TILE):
            x = scores[i * TILE:(i + 1) * TILE] * scale + addends[i]
            m = jnp.max(x, axis=1, keepdims=True)
            w = jnp.exp2(x - m)
            ls.append(jnp.sum(w, axis=1, keepdims=True))
            ms.append(m)
            ws.append(w.astype(BF16))
        return jnp.concatenate(ms, 0), jnp.concatenate(ls, 0), jnp.concatenate(ws, 0)

    def far(h):
        k = jnp.concatenate([kv[h, 2 * i + facing, 0] for i in range(3)], 0)
        v = jnp.concatenate([kv[h, 2 * i + facing, 1] for i in range(3)], 0)
        scores = lax.dot_general(fq[h], k, nt, preferred_element_type=F32)
        m, l, w = softmax(scores, HD, [fbias[pl.ds(2 * s + i, 1), :] for i in range(2)])
        ps[h, 0:HD, :] = jnp.dot(w, v, preferred_element_type=F32)
        lane = lax.broadcasted_iota(jnp.int32, (HD, HD), 1)
        ps[h, HD:HD + 8, :] = jnp.where(lane == 0, m, l).T[0:8, :]
        part(h).start()

    def near(h):
        k = kv[h, :, 0].reshape(6 * HD, HD)
        v = kv[h, :, 1].reshape(6 * HD, HD)
        scores = lax.dot_general(q2[h].reshape(2 * HD, HD), k, nt, preferred_element_type=F32)
        m, l, w = softmax(scores, 2 * HD, [bias[i:i + 1, :] for i in range(4)])
        accs[h] = jnp.dot(w, v, preferred_element_type=F32).reshape(2, HD, HD)
        peaks[h] = jnp.broadcast_to(m, (2 * HD, HD)).reshape(2, HD, HD)
        totals[h] = jnp.broadcast_to(l, (2 * HD, HD)).reshape(2, HD, HD)

    def keep_out(h):
        return pltpu.make_async_copy(o2.at[h, u], out.at[:, columns(u * half + h)], out_local.at[h])

    def give_out(h):
        return remote(o2.at[h, other], out.at[:, columns(u * half + h)], out_send.at[h], out_recv.at[h], dev(b, other))

    def got_out(h):
        return remote(o2.at[h, other], out.at[:, columns(other * half + h)], out_send.at[h], out_recv.at[h], dev(b, other))

    def merge(h):
        o2[h, s] = (accs[h, s] / totals[h, s]).astype(BF16)
        part(h).wait_recv()
        stats = jnp.concatenate([pr[h, HD:HD + 8, :]] * 16, 0).T
        m2, l2 = stats[:, 0:1], stats[:, 1:2]
        m1 = peaks[h, facing]
        m = jnp.maximum(m1, m2)
        a1, a2 = jnp.exp2(m1 - m), jnp.exp2(m2 - m)
        mixed = accs[h, facing] * a1 + pr[h, 0:HD, :] * a2
        o2[h, facing] = (mixed / (totals[h, facing] * a1 + l2 * a2)).astype(BF16)
        give_out(h).start()
        keep_out(h).start()

    def await_row(row, h):
        @pl.when(has_low)
        def _():
            got_kv(row, h).wait_recv()

        @pl.when(has_high)
        def _():
            got_kv(4 + row, h).wait_recv()

    def border(h):
        await_row(facing, h)
        to_across_q(0, h).wait_recv()
        far(h)

    def lead(h, carry):
        border(h)
        return carry

    def step(h, carry):
        @pl.when(h + LEAD < half)
        def _():
            border(h + LEAD)

        await_row(s, h)
        near(h)
        merge(h)
        return carry

    lax.fori_loop(0, LEAD, lead, 0)

    @pl.when(u != facing)
    def _():
        for h in range(half):
            for c in range(2):
                send_kv(c, h)

    lax.fori_loop(0, half, step, 0)

    to_across_keep().wait_send()
    to_partner_kv().wait_send()
    to_partner_q().wait_send()
    for h in range(half):
        for c in range(2):
            @pl.when(has_high)
            def _(c=c, h=h):
                to_high(c, h).wait_send()

            @pl.when(has_low)
            def _(c=c, h=h):
                to_low(c, h).wait_send()

            @pl.when(u == facing)
            def _(c=c, h=h):
                to_across_q(c, h).wait_send()

        part(h).wait_send()
        keep_out(h).wait()
        give_out(h).wait_send()
        got_out(h).wait_recv()


def body(query, key, value, keep):
    rows, width = query.shape
    heads = width // HD
    half = heads // 2
    frames = lax.axis_size("blk") // 2
    tiles, span = keep.shape
    dma = pltpu.SemaphoreType.DMA
    anywhere = pl.BlockSpec(memory_space=pl.ANY)
    scratch = [
        pltpu.VMEM((half, 6, 2, HD, HD), BF16),
        pltpu.VMEM((heads, 2, HD, HD), BF16),
        pltpu.VMEM((heads, HD, HD), BF16),
        pltpu.VMEM((half, 2, HD, HD), BF16),
        pltpu.VMEM((half, HD, HD), BF16),
        pltpu.VMEM((tiles, span), jnp.int32),
        pltpu.VMEM((tiles, 6 * HD), F32),
        pltpu.VMEM((tiles, 3 * HD), F32),
        pltpu.VMEM((half, HD + 8, HD), F32),
        pltpu.VMEM((half, HD + 8, HD), F32),
        pltpu.VMEM((half, 2, HD, HD), F32),
        pltpu.VMEM((half, 2, HD, HD), F32),
        pltpu.VMEM((half, 2, HD, HD), F32),
        pltpu.VMEM((half, 2, HD, HD), BF16),
        dma((heads, 2)),
        dma((heads,)),
        dma((half, 2)),
        dma((half,)),
        dma((6, half)),
        dma((2, 2, half)),
        dma((2,)),
        dma((1,)),
        dma((1,)),
        dma((2, half)),
        dma((half,)),
        dma((1,)),
        dma((1,)),
        dma((half,)),
        dma((half,)),
        dma((half,)),
        dma((half,)),
        dma((half,)),
    ]
    return pl.pallas_call(
        functools.partial(kernel, heads, frames),
        out_shape=jax.ShapeDtypeStruct((rows, width), BF16),
        in_specs=[anywhere, anywhere, anywhere, pl.BlockSpec(memory_space=pltpu.VMEM)],
        out_specs=anywhere,
        scratch_shapes=scratch,
        compiler_params=pltpu.CompilerParams(
            collective_id=0, has_side_effects=True, vmem_limit_bytes=56 * 1024 * 1024),
    )(query, key, value, keep)


def solution(mesh):
    return jax.shard_map(
        body,
        mesh=mesh,
        in_specs=(
            P(("groups", "blk", "uly"), None),
            P(("groups", "blk", "uly"), None),
            P(("groups", "blk", "uly"), None),
            P(("groups", "blk"), None),
        ),
        out_specs=P(("groups", "blk", "uly"), None),
        check_vma=False,
    )
```

```python
import functools
import math

import jax
import jax.numpy as jnp
from jax import lax
from jax.experimental import pallas as pl
from jax.experimental.pallas import tpu as pltpu
from jax.sharding import PartitionSpec as P

HD = 128
TILE = 64
FAR = 1e30
LEAD = 4
F32 = jnp.float32
BF16 = jnp.bfloat16
MESH = pl.DeviceIdType.MESH


def kernel(heads, frames, query, key, value, keep, out,
           kv, kvs, qs, q2, fq, fkeep, bias, fbias, ps, pr, accs, peaks, totals, o2,
           sem_kvs, sem_qs, sem_own, sem_own_q, recv_kv, zsend, psend, pqsend, recv_q2,
           fqsend, recv_fq, ksend, recv_keep, part_send, part_recv, out_local, out_send, out_recv):
    half = heads // 2
    group = lax.axis_index("groups")
    b = lax.axis_index("blk")
    u = lax.axis_index("uly")
    t = b // 2
    s = b - 2 * t
    other = 1 - u
    facing = 1 - s
    across = b + 1 - 2 * s
    has_low = t > 0
    has_high = t < frames - 1

    def dev(blk, core):
        return (group, blk, core)

    def remote(src, dst, send, recv, device):
        return pltpu.make_async_remote_copy(
            src_ref=src, dst_ref=dst, send_sem=send, recv_sem=recv,
            device_id=device, device_id_type=MESH)

    def columns(head):
        return pl.ds(pl.multiple_of(head * HD, HD), HD)

    def load_key(hd):
        return pltpu.make_async_copy(key.at[:, columns(hd)], kvs.at[hd, 0], sem_kvs.at[hd, 0])

    def load_value(hd):
        return pltpu.make_async_copy(value.at[:, columns(hd)], kvs.at[hd, 1], sem_kvs.at[hd, 1])

    def load_query(hd):
        return pltpu.make_async_copy(query.at[:, columns(hd)], qs.at[hd], sem_qs.at[hd])

    def own_kv(h):
        return (
            pltpu.make_async_copy(key.at[:, columns(u * half + h)], kv.at[h, 2 + u, 0], sem_own.at[h, 0]),
            pltpu.make_async_copy(value.at[:, columns(u * half + h)], kv.at[h, 2 + u, 1], sem_own.at[h, 1]),
        )

    def own_q(h):
        return pltpu.make_async_copy(query.at[:, columns(u * half + h)], q2.at[h, u], sem_own_q.at[h])

    for h in range(half):
        for c in range(2):
            load_key(c * half + h).start()
            load_value(c * half + h).start()
            load_query(c * half + h).start()
    for h in range(half):
        for copy in own_kv(h):
            copy.start()
        own_q(h).start()

    def to_high(c, h):
        return remote(kvs.at[c * half + h], kv.at[h, u], zsend.at[0, c, h], recv_kv.at[u, h], dev(b + 2, c))

    def to_low(c, h):
        return remote(kvs.at[c * half + h], kv.at[h, 4 + u], zsend.at[1, c, h], recv_kv.at[4 + u, h], dev(b - 2, c))

    def got_kv(row, h):
        return remote(kvs.at[h], kv.at[h, row], zsend.at[0, 0, h], recv_kv.at[row, h], dev(b, other))

    def to_partner_kv():
        return remote(kvs.at[pl.ds(other * half, half)], kv.at[:, 2 + u], psend.at[0], psend.at[1], dev(b, other))

    def got_partner_kv():
        return remote(kvs.at[pl.ds(other * half, half)], kv.at[:, 2 + other], psend.at[0], psend.at[1], dev(b, other))

    def to_partner_q():
        return remote(qs.at[pl.ds(other * half, half)], q2.at[:, u], pqsend.at[0], recv_q2.at[0], dev(b, other))

    def got_partner_q():
        return remote(qs.at[pl.ds(other * half, half)], q2.at[:, other], pqsend.at[0], recv_q2.at[0], dev(b, other))

    def to_across_q(c, h):
        return remote(qs.at[c * half + h], fq.at[h], fqsend.at[c, h], recv_fq.at[h], dev(across, c))

    def to_across_keep():
        return remote(keep, fkeep, ksend.at[0], recv_keep.at[0], dev(across, u))

    def part(h):
        return remote(ps.at[h], pr.at[h], part_send.at[h], part_recv.at[h], dev(across, u))

    barrier = pltpu.get_barrier_semaphore()

    def greet(blk, core):
        pl.semaphore_signal(barrier, inc=1, device_id=dev(blk, core), device_id_type=MESH)

    greet(b, other)
    for c in range(2):
        greet(across, c)

        @pl.when(has_low)
        def _(c=c):
            greet(b - 2, c)

        @pl.when(has_high)
        def _(c=c):
            greet(b + 2, c)

    @pl.when(jnp.logical_not(has_low))
    def _():
        kv[:, 0:2] = jnp.zeros((half, 2, 2, HD, HD), BF16)

    @pl.when(jnp.logical_not(has_high))
    def _():
        kv[:, 4:6] = jnp.zeros((half, 2, 2, HD, HD), BF16)

    around = jnp.where(has_low, 2, 0) + jnp.where(has_high, 2, 0)
    pl.semaphore_wait(barrier, 3 + around)

    def send_kv(c, h):
        @pl.when(has_high)
        def _():
            to_high(c, h).start()

        @pl.when(has_low)
        def _():
            to_low(c, h).start()

    to_across_keep().start()
    for h in range(half):
        for c in range(2):
            load_key(c * half + h).wait()
            load_value(c * half + h).wait()

            @pl.when(u == facing)
            def _(c=c, h=h):
                send_kv(c, h)

            load_query(c * half + h).wait()

            @pl.when(u == facing)
            def _(c=c, h=h):
                to_across_q(c, h).start()

    to_partner_kv().start()
    to_partner_q().start()
    for h in range(half):
        for copy in own_kv(h):
            copy.wait()
        own_q(h).wait()

    wide = keep.shape[1]
    tiles_here = keep.shape[0]
    reach = (wide // tiles_here - 1) // 2

    def addend(flags, column, count):
        lanes = lax.broadcasted_iota(jnp.int32, (wide, count), 1)
        chosen = lax.broadcasted_iota(jnp.int32, (wide, count), 0) == column(lanes)
        picked = jnp.dot(flags.astype(F32).astype(BF16), chosen.astype(F32).astype(BF16), preferred_element_type=F32)
        return jnp.where(picked > 0.5, 0.0, -FAR)

    def own_column(lanes):
        row = lanes // HD
        return (tiles_here * (reach - 2) + 2 * tiles_here * (row // 2)
                + 2 * (row % 2) + (lanes % HD) // TILE)

    def far_column(lanes):
        return (tiles_here * (reach - 2 + 2 * s - 1) + 2 * tiles_here * (lanes // HD)
                + 2 * facing + (lanes % HD) // TILE)

    bias[...] = addend(keep[...], own_column, 6 * HD)
    remote(keep, fkeep, ksend.at[0], recv_keep.at[0], dev(across, u)).wait_recv()
    fbias[...] = addend(fkeep[...], far_column, 3 * HD)

    got_partner_kv().wait_recv()
    got_partner_q().wait_recv()

    scale = math.log2(math.e) / math.sqrt(HD)
    nt = (((1,), (1,)), ((), ()))

    def softmax(scores, rows, addends):
        ms, ls, ws = [], [], []
        for i in range(rows // TILE):
            x = scores[i * TILE:(i + 1) * TILE] * scale + addends[i]
            m = jnp.max(x, axis=1, keepdims=True)
            w = jnp.exp2(x - m)
            ls.append(jnp.sum(w, axis=1, keepdims=True))
            ms.append(m)
            ws.append(w.astype(BF16))
        return jnp.concatenate(ms, 0), jnp.concatenate(ls, 0), jnp.concatenate(ws, 0)

    def far(h):
        k = jnp.concatenate([kv[h, 2 * i + facing, 0] for i in range(3)], 0)
        v = jnp.concatenate([kv[h, 2 * i + facing, 1] for i in range(3)], 0)
        scores = lax.dot_general(fq[h], k, nt, preferred_element_type=F32)
        m, l, w = softmax(scores, HD, [fbias[pl.ds(2 * s + i, 1), :] for i in range(2)])
        ps[h, 0:HD, :] = jnp.dot(w, v, preferred_element_type=F32)
        lane = lax.broadcasted_iota(jnp.int32, (HD, HD), 1)
        ps[h, HD:HD + 8, :] = jnp.where(lane == 0, m, l).T[0:8, :]
        part(h).start()

    def near(h):
        k = kv[h, :, 0].reshape(6 * HD, HD)
        v = kv[h, :, 1].reshape(6 * HD, HD)
        scores = lax.dot_general(q2[h].reshape(2 * HD, HD), k, nt, preferred_element_type=F32)
        m, l, w = softmax(scores, 2 * HD, [bias[i:i + 1, :] for i in range(4)])
        accs[h] = jnp.dot(w, v, preferred_element_type=F32).reshape(2, HD, HD)
        peaks[h] = jnp.broadcast_to(m, (2 * HD, HD)).reshape(2, HD, HD)
        totals[h] = jnp.broadcast_to(l, (2 * HD, HD)).reshape(2, HD, HD)

    def keep_out(h):
        return pltpu.make_async_copy(o2.at[h, u], out.at[:, columns(u * half + h)], out_local.at[h])

    def give_out(h):
        return remote(o2.at[h, other], out.at[:, columns(u * half + h)], out_send.at[h], out_recv.at[h], dev(b, other))

    def got_out(h):
        return remote(o2.at[h, other], out.at[:, columns(other * half + h)], out_send.at[h], out_recv.at[h], dev(b, other))

    def merge(h):
        o2[h, s] = (accs[h, s] / totals[h, s]).astype(BF16)
        part(h).wait_recv()
        stats = jnp.concatenate([pr[h, HD:HD + 8, :]] * 16, 0).T
        m2, l2 = stats[:, 0:1], stats[:, 1:2]
        m1 = peaks[h, facing]
        m = jnp.maximum(m1, m2)
        a1, a2 = jnp.exp2(m1 - m), jnp.exp2(m2 - m)
        mixed = accs[h, facing] * a1 + pr[h, 0:HD, :] * a2
        o2[h, facing] = (mixed / (totals[h, facing] * a1 + l2 * a2)).astype(BF16)
        give_out(h).start()
        keep_out(h).start()

    def await_row(row, h):
        @pl.when(has_low)
        def _():
            got_kv(row, h).wait_recv()

        @pl.when(has_high)
        def _():
            got_kv(4 + row, h).wait_recv()

    def border(h):
        await_row(facing, h)
        to_across_q(0, h).wait_recv()
        far(h)

    def lead(h, carry):
        border(h)
        return carry

    def step(h, carry):
        @pl.when(h + LEAD < half)
        def _():
            border(h + LEAD)

        await_row(s, h)
        near(h)
        merge(h)
        return carry

    lax.fori_loop(0, LEAD, lead, 0)

    @pl.when(u != facing)
    def _():
        for h in range(half):
            for c in range(2):
                send_kv(c, h)

    lax.fori_loop(0, half, step, 0)

    to_across_keep().wait_send()
    to_partner_kv().wait_send()
    to_partner_q().wait_send()
    for h in range(half):
        for c in range(2):
            @pl.when(has_high)
            def _(c=c, h=h):
                to_high(c, h).wait_send()

            @pl.when(has_low)
            def _(c=c, h=h):
                to_low(c, h).wait_send()

            @pl.when(u == facing)
            def _(c=c, h=h):
                to_across_q(c, h).wait_send()

        part(h).wait_send()
        keep_out(h).wait()
        give_out(h).wait_send()
        got_out(h).wait_recv()


def body(query, key, value, keep):
    rows, width = query.shape
    heads = width // HD
    half = heads // 2
    frames = lax.axis_size("blk") // 2
    tiles, span = keep.shape
    dma = pltpu.SemaphoreType.DMA
    anywhere = pl.BlockSpec(memory_space=pl.ANY)
    scratch = [
        pltpu.VMEM((half, 6, 2, HD, HD), BF16),
        pltpu.VMEM((heads, 2, HD, HD), BF16),
        pltpu.VMEM((heads, HD, HD), BF16),
        pltpu.VMEM((half, 2, HD, HD), BF16),
        pltpu.VMEM((half, HD, HD), BF16),
        pltpu.VMEM((tiles, span), jnp.int32),
        pltpu.VMEM((tiles, 6 * HD), F32),
        pltpu.VMEM((tiles, 3 * HD), F32),
        pltpu.VMEM((half, HD + 8, HD), F32),
        pltpu.VMEM((half, HD + 8, HD), F32),
        pltpu.VMEM((half, 2, HD, HD), F32),
        pltpu.VMEM((half, 2, HD, HD), F32),
        pltpu.VMEM((half, 2, HD, HD), F32),
        pltpu.VMEM((half, 2, HD, HD), BF16),
        dma((heads, 2)),
        dma((heads,)),
        dma((half, 2)),
        dma((half,)),
        dma((6, half)),
        dma((2, 2, half)),
        dma((2,)),
        dma((1,)),
        dma((1,)),
        dma((2, half)),
        dma((half,)),
        dma((1,)),
        dma((1,)),
        dma((half,)),
        dma((half,)),
        dma((half,)),
        dma((half,)),
        dma((half,)),
    ]
    return pl.pallas_call(
        functools.partial(kernel, heads, frames),
        out_shape=pltpu.VMEM((rows, width), BF16),
        in_specs=[anywhere, anywhere, anywhere, pl.BlockSpec(memory_space=pltpu.VMEM)],
        out_specs=pl.BlockSpec(memory_space=pltpu.VMEM),
        scratch_shapes=scratch,
        compiler_params=pltpu.CompilerParams(
            collective_id=0, has_side_effects=True, vmem_limit_bytes=56 * 1024 * 1024),
    )(query, key, value, keep)


def solution(mesh):
    return jax.shard_map(
        body,
        mesh=mesh,
        in_specs=(
            P(("groups", "blk", "uly"), None),
            P(("groups", "blk", "uly"), None),
            P(("groups", "blk", "uly"), None),
            P(("groups", "blk"), None),
        ),
        out_specs=P(("groups", "blk", "uly"), None),
        check_vma=False,
    )
```
